512 devices in a mesh: role: 4 (over y), rows: 128 (over x, z, core).
Axes of the slice: x: 4, y: 4, z: 16, core: 2. Of those that a mesh axis runs over, the one named last changes fastest.
Arguments:
- embeddings: float32 [32768, 1024], P('rows'), may hold values from -6 to 6
- earlier_factor: float32 [32768, 256], P('rows', 'role'), may hold values from -0.5 to 0.5
- block_of: int32 [128], replicated, may hold values from 0 to 127, each once
Outputs:
- factor_panels: float32 [32768, 2, 256], P('rows', None, 'role')
The draws below stay inside these ranges and needn't reach their ends.
Inputs may be any that keep to these rules, and one draw needn't show every extreme that they name: `block_of`: a permutation: each matrix row block 0 to 127 sits at exactly one stored block position.
All inputs are finite; a program needn't handle non-finite values.
Results may differ from the reference program's by a relative error of at most 0.0003.
Values sent between devices are 32-bit elements; how exact they have to be, the bound alone decides.
No kernel may reach another device: no remote copies, remote signals or barrier semaphores. Data moves between devices by JAX's collectives and lax.ppermute only.
A program may use at most 64 MiB of HBM per device.

```python
import math
import jax
import jax.numpy as jnp
from jax import lax

B = 256
F = 1024
PREV = 256
NBLK = 128
M = 32768


def draw_earlier_factor(key, part):
    key_common = jax.random.fold_in(key, 11)
    key_noise = jax.random.fold_in(key, 12)
    spread = 0.2 / (math.sqrt(PREV) + math.sqrt(2 * B)) ** 2
    common_size = 0.03 / B
    noise = jax.random.normal(key_noise, (M, PREV), jnp.float32)
    direction = jax.random.normal(key_common, (PREV,), jnp.float32)
    common = direction * (math.sqrt(common_size) / jnp.sqrt(jnp.sum(direction * direction)))
    values = common[None, :] + noise * math.sqrt(spread)
    return jnp.clip(values, -0.5, 0.5).astype(jnp.float32)


def block_levels(own_key, extent, split, low, top_value):
    factor_of, own = 1.0, jax.random.fold_in(own_key, 6)
    for position, blocks in split:
        draws = jnp.exp(jax.random.uniform(jax.random.fold_in(own, position), (blocks,), jnp.float32, low / len(split), top_value / len(split)))
        factor_of = factor_of * jnp.repeat(draws, extent[position] // blocks).reshape([-1 if axis == position else 1 for axis in range(len(extent))])
    return factor_of


def bell_draw(rng, dims, deviation, most, cuts=(), kind=jnp.bfloat16):
    array = deviation * jax.random.normal(rng, dims, jnp.float32)
    if cuts:
        array = array * block_levels(rng, dims, cuts, -0.22, 0.18)
    return jnp.clip(array, -most, most).astype(kind)


def setup_inputs(seed: int = 0) -> dict:
    arg_keys = jax.random.split(jax.random.key(seed), 4)
    return {
        "embeddings": bell_draw(arg_keys[0], (M, F), 1.0, 6.0, ((0, 128),), jnp.float32),
        "earlier_factor": draw_earlier_factor(jax.random.fold_in(arg_keys[3], 71), 0),
        "block_of": jax.random.permutation(arg_keys[2], NBLK).astype(jnp.int32),
    }


highest = lax.Precision.HIGHEST

def reference(embeddings, earlier_factor, block_of):
    total_rows = embeddings.shape[0]
    block_count = total_rows // B
    slot_ids = jnp.arange(block_count, dtype=jnp.int32)
    row_block = jnp.repeat(block_of, B, total_repeat_length=total_rows)
    local_row = jnp.arange(total_rows, dtype=jnp.int32) % B
    column_ids = jnp.arange(B, dtype=jnp.int32)
    row_norms = jnp.sum(embeddings * embeddings, axis=1)
    factor_known = earlier_factor
    results = []
    for panel in range(2):
        owner_slot = jnp.sum(jnp.where(block_of == panel, slot_ids, 0)).astype(jnp.int32)
        start = (owner_slot * B).astype(jnp.int32)
        panel_points = lax.dynamic_slice_in_dim(embeddings, start, B, 0)
        known_rows = lax.dynamic_slice_in_dim(factor_known, start, B, 0)
        col_norms = jnp.sum(panel_points * panel_points, axis=1)
        inner_products = jnp.dot(embeddings.astype(jnp.float32), panel_points.T.astype(jnp.float32), precision=highest, preferred_element_type=jnp.float32)
        kernel = jnp.exp(-(row_norms[:, None] + col_norms[None, :] - 2.0 * inner_products) / (2.0 * F))
        update = jnp.dot(factor_known.astype(jnp.float32), known_rows.T.astype(jnp.float32), precision=highest, preferred_element_type=jnp.float32)
        ridge = jnp.where((row_block[:, None] == panel) & (local_row[:, None] == column_ids[None, :]), 1.0, 0.0)
        schur_rows = kernel - update + ridge
        diag_block = lax.dynamic_slice_in_dim(schur_rows, start, B, 0)
        lower_factor = jnp.linalg.cholesky(diag_block)
        inverse = jax.scipy.linalg.solve_triangular(lower_factor, jnp.eye(B, dtype=jnp.float32), lower=True)
        factor_piece = jnp.dot(schur_rows.astype(jnp.float32), inverse.T.astype(jnp.float32), precision=highest, preferred_element_type=jnp.float32)
        factor_piece = jnp.where((row_block < panel)[:, None], 0.0, factor_piece)
        results.append(factor_piece)
        factor_known = jnp.concatenate([factor_known, factor_piece], axis=1)
    return jnp.stack(results, axis=1)
```

```python
import jax
import jax.numpy as jnp
from jax import lax
from jax.sharding import Mesh
from jax.sharding import PartitionSpec as P

ROWS = ("x", "z", "core")

highest = lax.Precision.HIGHEST
ridge_weight = 1.0


def outer_rows(rows, columns):
    return lax.dot_general(
        rows,
        columns,
        (((1,), (1,)), ((), ())),
        precision=highest,
        preferred_element_type=jnp.float32,
    )


def exchange(array, axis):
    return lax.all_to_all(array, axis, 0, 0, tiled=True)


def copies_from(array, axis):
    count = lax.axis_size(axis)
    return exchange(jnp.broadcast_to(array[None], (count, *array.shape)), axis)


def pick(array, index):
    return lax.dynamic_index_in_dim(array, index, 0, keepdims=False)


def broadcast_panels(payload, owners):
    z_count = lax.axis_size("z")
    rows, width = payload.shape
    groups = rows // 8
    halves = z_count // groups
    pieces = payload.reshape(groups, 8, halves, width // halves)
    pieces = pieces.transpose(0, 2, 1, 3).reshape(z_count, 8, width // halves)
    seen = exchange(pieces, "z")
    x_count, core_count = lax.axis_size("x"), lax.axis_size("core")
    candidates = jnp.stack(
        [pick(seen, (owner // core_count) % z_count) for owner in owners]
    )
    wide = jnp.broadcast_to(candidates[None], (x_count, *candidates.shape))
    wide = wide.reshape(x_count * core_count, *candidates.shape[1:])
    seen = exchange(wide, ("x", "core"))
    own = jnp.where(lax.axis_index("core") == 0, owners[0], owners[1])
    source = own // (z_count * core_count) * core_count + own % core_count
    piece = pick(seen, source)
    return lax.all_gather(piece, "z", axis=0)


def kernel_of(row_points, row_norms, col_points, col_norms, scale):
    inner = outer_rows(row_points, col_points)
    return jnp.exp(-(row_norms[:, None] + col_norms[None, :] - 2.0 * inner) / scale)


def ridge(size):
    return ridge_weight * jnp.eye(size, dtype=jnp.float32)


def factor_inverse(diag_block):
    size = diag_block.shape[0]
    lower_factor = jnp.linalg.cholesky(diag_block)
    return jax.scipy.linalg.solve_triangular(
        lower_factor, jnp.eye(size, dtype=jnp.float32), lower=True
    )


def on_device(embeddings, earlier_factor, block_of):
    size, width = embeddings.shape
    role_count = lax.axis_size("role")
    columns = size // role_count
    role = lax.axis_index("role")
    slot = lax.axis_index(ROWS)
    my_block = lax.dynamic_index_in_dim(block_of, slot, 0, keepdims=False)
    slots = jnp.arange(block_of.shape[0], dtype=jnp.int32)
    owners = [jnp.sum(jnp.where(block_of == panel, slots, 0)) for panel in range(2)]

    own_points = lax.dynamic_slice_in_dim(embeddings, role * columns, columns, 0)
    known_wide = jnp.concatenate(
        [earlier_factor[g * columns : (g + 1) * columns] for g in range(role_count)], axis=1
    )
    payload = jnp.concatenate([own_points, known_wide], axis=1)
    quarter = broadcast_panels(payload, owners)
    mine = copies_from(quarter, "role")
    known = copies_from(earlier_factor, "role")
    known = known.transpose(1, 0, 2).reshape(size, size)
    other = lax.ppermute(mine, "core", [(0, 1), (1, 0)])
    first = lax.axis_index("core") == 0
    panels = (jnp.where(first, mine, other), jnp.where(first, other, mine))

    points, knowns = [], []
    groups = columns // 8
    for panel in panels:
        halves = panel.shape[1] // groups
        whole = panel.reshape(role_count, groups, halves, 8, -1).transpose(0, 1, 3, 2, 4)
        whole = whole.reshape(size, -1)
        points.append(whole[:, :width])
        part = whole[:, width:].reshape(role_count, columns, role_count, columns)
        knowns.append(part.transpose(2, 1, 0, 3).reshape(size, size))

    scale = 2.0 * width
    norms = [jnp.sum(p * p, axis=1) for p in points]
    row_norms = jnp.sum(embeddings * embeddings, axis=1)

    def schur(rows, rows_norm, rows_known, panel):
        kernel = kernel_of(rows, rows_norm, points[panel], norms[panel], scale)
        return kernel - outer_rows(rows_known, knowns[panel])

    first_rows = schur(embeddings, row_norms, known, 0) + jnp.where(my_block == 0, ridge(size), 0.0)
    second_rows = schur(embeddings, row_norms, known, 1) + jnp.where(my_block == 1, ridge(size), 0.0)
    top = schur(points[0], norms[0], knowns[0], 0) + ridge(size)
    side = schur(points[1], norms[1], knowns[1], 0)
    low = schur(points[1], norms[1], knowns[1], 1) + ridge(size)

    top_inverse = factor_inverse(top)
    below = outer_rows(side, top_inverse)
    low_inverse = factor_inverse(low - outer_rows(below, below))
    first_panel = outer_rows(first_rows, top_inverse)
    second_rows = second_rows - outer_rows(first_panel, below)
    own_inverse = lax.dynamic_slice_in_dim(low_inverse, role * columns, columns, 0)
    second_panel = outer_rows(second_rows, own_inverse)
    second_panel = jnp.where(my_block < 1, 0.0, second_panel)
    first_panel = lax.dynamic_slice_in_dim(first_panel, role * columns, columns, 1)
    return jnp.stack([first_panel, second_panel], axis=1)


def solution(mesh):
    shape = mesh.shape
    finer = Mesh(
        mesh.devices.reshape(shape["role"], 4, 16, 2), ("role", *ROWS)
    )
    placed = (P(ROWS, None), P(ROWS, "role"), P())
    return jax.shard_map(
        on_device, mesh=finer, in_specs=placed, out_specs=P(ROWS, None, "role"), check_vma=False
    )
```

```python
import jax
import jax.numpy as jnp
from jax import lax
from jax.experimental import pallas as pl
from jax.sharding import Mesh
from jax.sharding import PartitionSpec as P

ROWS = ("x", "far", "near", "core")

highest = lax.Precision.HIGHEST
ridge_weight = 1.0
TILE = 64
STEP = 8


def outer_rows(rows, columns):
    return lax.dot_general(
        rows,
        columns,
        (((1,), (1,)), ((), ())),
        precision=highest,
        preferred_element_type=jnp.float32,
    )


def product(left, right):
    return lax.dot_general(
        left,
        right,
        (((1,), (0,)), ((), ())),
        precision=highest,
        preferred_element_type=jnp.float32,
    )


def exchange(array, axis):
    return lax.all_to_all(array, axis, 0, 0, tiled=True)


def copies_from(array, axis):
    count = lax.axis_size(axis)
    return exchange(jnp.broadcast_to(array[None], (count, *array.shape)), axis)


def pick(array, index):
    return lax.dynamic_index_in_dim(array, index, 0, keepdims=False)


def small_inverse(block):
    size = block.shape[0]
    row_ids = lax.broadcasted_iota(jnp.int32, (size, size), 0)
    col_ids = lax.broadcasted_iota(jnp.int32, (size, size), 1)
    identity = (row_ids == col_ids).astype(jnp.float32)
    both = jnp.concatenate([block, identity], axis=1)
    tiles = [both[STEP * g : STEP * g + STEP] for g in range(size // STEP)]
    shape = tiles[0].shape
    lane = lax.broadcasted_iota(jnp.int32, shape, 0)
    pivots = [None] * len(tiles)
    for g in range(len(tiles)):
        later = range(g, len(tiles))
        start = STEP * g
        cols = [
            {h: jnp.broadcast_to(tiles[h][:, start + q : start + q + 1], shape) for h in later}
            for q in range(STEP)
        ]
        rows = [jnp.broadcast_to(tiles[g][a : a + 1], shape) for a in range(STEP)]
        piv = [
            [jnp.broadcast_to(cols[b][g][a : a + 1], shape) for b in range(a + 1)]
            for a in range(STEP)
        ]
        inverse = [None] * STEP
        for q in range(STEP):
            if q % 2 == 0:
                inverse[q] = 1.0 / piv[q][q]
                inverse[q + 1] = piv[q][q] / (
                    piv[q][q] * piv[q + 1][q + 1] - piv[q + 1][q] * piv[q + 1][q]
                )
            for a in range(q + 1, STEP):
                ratio = piv[a][q] * inverse[q]
                for b in range(q + 1, a + 1):
                    piv[a][b] = piv[a][b] - ratio * piv[b][q]
                rows[a] = rows[a] - ratio * rows[q]
                for h in later:
                    cols[a][h] = cols[a][h] - ratio * cols[q][h]
        pivots[g] = piv[0][0]
        for q in range(1, STEP):
            pivots[g] = jnp.where(lane == q, piv[q][q], pivots[g])
        for h in later:
            for q in range(STEP):
                if h == g and q == STEP - 1:
                    continue
                factor = cols[q][h] * inverse[q]
                if h == g:
                    factor = jnp.where(lane > q, factor, 0.0)
                tiles[h] = tiles[h] - factor * rows[q]
    done = [t[:, size:] * lax.rsqrt(p[:, size:]) for t, p in zip(tiles, pivots)]
    return jnp.concatenate(done, axis=0)


def factor_inverse(whole):
    count = whole.shape[0] // TILE
    left = [
        [whole[TILE * i : TILE * i + TILE, TILE * j : TILE * j + TILE] for j in range(count)]
        for i in range(count)
    ]
    lower = [[None] * count for _ in range(count)]
    inverse = [[jnp.zeros((TILE, TILE), jnp.float32)] * count for _ in range(count)]
    for k in range(count):
        inverse[k][k] = small_inverse(left[k][k])
        for i in range(k + 1, count):
            lower[i][k] = outer_rows(left[i][k], inverse[k][k])
        for i in range(k + 1, count):
            for j in range(k + 1, i + 1):
                left[i][j] = left[i][j] - outer_rows(lower[i][k], lower[j][k])
        for j in range(k):
            total = product(lower[k][j], inverse[j][j])
            for m in range(j + 1, k):
                total = total + product(lower[k][m], inverse[m][j])
            inverse[k][j] = -product(inverse[k][k], total)
    return jnp.concatenate([jnp.concatenate(row, axis=1) for row in inverse], axis=0)


def factor_kernel(top_ref, side_ref, low_ref, first_ref, below_ref, second_ref):
    first = factor_inverse(top_ref[...])
    first_ref[...] = first
    below = outer_rows(side_ref[...], first)
    below_ref[...] = below
    second_ref[...] = factor_inverse(low_ref[...] - outer_rows(below, below))


def factors(top, side, low):
    square = jax.ShapeDtypeStruct(top.shape, jnp.float32)
    return pl.pallas_call(
        factor_kernel, out_shape=(square, square, square), name="factors"
    )(top, side, low)


def broadcast_panels(payload, owners):
    far_count, near_count = lax.axis_size("far"), lax.axis_size("near")
    x_count, core_count = lax.axis_size("x"), lax.axis_size("core")
    role_count = lax.axis_size("role")
    rows, width = payload.shape
    groups = near_count * x_count
    high, half = rows // groups, width // core_count
    pieces = payload.reshape(groups, high, core_count, half)
    pieces = pieces.transpose(0, 2, 1, 3).reshape(groups * core_count, high, half)
    seen = exchange(pieces, ("near", "x", "core"))
    sources, fars = [], []
    for owner in owners:
        core, place = owner % core_count, owner // core_count
        near, place = place % near_count, place // near_count
        far, x = place % far_count, place // far_count
        sources.append((near * x_count + x) * core_count + core)
        fars.append(far)
    own = jnp.stack([pick(seen, source) for source in sources])
    seen = copies_from(own.reshape(-1, half), "far").reshape(far_count, *own.shape)
    own = jnp.stack([pick(seen[:, p], far) for p, far in enumerate(fars)])
    strip = copies_from(own.reshape(-1, half), "near")
    mine = copies_from(strip, ("role", "x"))
    other = lax.ppermute(mine, "core", [(0, 1), (1, 0)])
    first = lax.axis_index("core") == 0
    both = jnp.stack([jnp.where(first, mine, other), jnp.where(first, other, mine)])
    both = both.reshape(core_count, role_count, x_count, near_count, len(owners), high, half)
    both = both.transpose(4, 1, 3, 2, 5, 0, 6)
    return both.reshape(len(owners), role_count * rows, width)


def kernel_of(row_points, row_norms, col_points, col_norms, scale):
    inner = outer_rows(row_points, col_points)
    return jnp.exp(-(row_norms[:, None] + col_norms[None, :] - 2.0 * inner) / scale)


def ridge(size):
    return ridge_weight * jnp.eye(size, dtype=jnp.float32)


def on_device(embeddings, earlier_factor, block_of):
    size, width = embeddings.shape
    role_count = lax.axis_size("role")
    columns = size // role_count
    role = lax.axis_index("role")
    slot = lax.axis_index(ROWS)
    my_block = lax.dynamic_index_in_dim(block_of, slot, 0, keepdims=False)
    slots = jnp.arange(block_of.shape[0], dtype=jnp.int32)
    owners = [jnp.sum(jnp.where(block_of == panel, slots, 0)) for panel in range(2)]

    own_points = lax.dynamic_slice_in_dim(embeddings, role * columns, columns, 0)
    known_wide = jnp.concatenate(
        [earlier_factor[g * columns : (g + 1) * columns] for g in range(role_count)], axis=1
    )
    payload = jnp.concatenate([own_points, known_wide], axis=1)
    panels = broadcast_panels(payload, owners)
    known = copies_from(earlier_factor, "role")
    known = known.transpose(1, 0, 2).reshape(size, size)

    points, knowns = [], []
    for panel in panels:
        points.append(panel[:, :width])
        part = panel[:, width:].reshape(role_count, columns, role_count, columns)
        knowns.append(part.transpose(2, 1, 0, 3).reshape(size, size))

    scale = 2.0 * width
    norms = [jnp.sum(p * p, axis=1) for p in points]
    row_norms = jnp.sum(embeddings * embeddings, axis=1)

    def schur(rows, rows_norm, rows_known, panel):
        kernel = kernel_of(rows, rows_norm, points[panel], norms[panel], scale)
        return kernel - outer_rows(rows_known, knowns[panel])

    first_rows = schur(embeddings, row_norms, known, 0) + jnp.where(my_block == 0, ridge(size), 0.0)
    second_rows = schur(embeddings, row_norms, known, 1) + jnp.where(my_block == 1, ridge(size), 0.0)
    top = schur(points[0], norms[0], knowns[0], 0) + ridge(size)
    side = schur(points[1], norms[1], knowns[1], 0)
    low = schur(points[1], norms[1], knowns[1], 1) + ridge(size)

    top_inverse, below, low_inverse = factors(top, side, low)
    first_panel = outer_rows(first_rows, top_inverse)
    second_rows = second_rows - outer_rows(first_panel, below)
    own_inverse = lax.dynamic_slice_in_dim(low_inverse, role * columns, columns, 0)
    second_panel = outer_rows(second_rows, own_inverse)
    second_panel = jnp.where(my_block < 1, 0.0, second_panel)
    first_panel = lax.dynamic_slice_in_dim(first_panel, role * columns, columns, 1)
    return jnp.stack([first_panel, second_panel], axis=1)


def solution(mesh):
    finer = Mesh(
        mesh.devices.reshape(mesh.shape["role"], 4, 4, 4, 2), ("role", *ROWS)
    )
    placed = (P(ROWS, None), P(ROWS, "role"), P())
    return jax.shard_map(
        on_device, mesh=finer, in_specs=placed, out_specs=P(ROWS, None, "role"), check_vma=False
    )
```

```python
import jax
import jax.numpy as jnp
from jax import lax
from jax.experimental import pallas as pl
from jax.experimental.pallas import tpu as pltpu
from jax.sharding import Mesh
from jax.sharding import PartitionSpec as P

ROWS = ("x", "far", "near", "core")

highest = lax.Precision.HIGHEST
ridge_weight = 1.0
TILE = 64
STEP = 8


def outer_rows(rows, columns):
    return lax.dot_general(
        rows,
        columns,
        (((1,), (1,)), ((), ())),
        precision=highest,
        preferred_element_type=jnp.float32,
    )


def product(left, right):
    return lax.dot_general(
        left,
        right,
        (((1,), (0,)), ((), ())),
        precision=highest,
        preferred_element_type=jnp.float32,
    )


def exchange(array, axis):
    return lax.all_to_all(array, axis, 0, 0, tiled=True)


def copies_from(array, axis):
    count = lax.axis_size(axis)
    return exchange(jnp.broadcast_to(array[None], (count, *array.shape)), axis)


def pick(array, index):
    return lax.dynamic_index_in_dim(array, index, 0, keepdims=False)


def small_inverse(block):
    size = block.shape[0]
    row_ids = lax.broadcasted_iota(jnp.int32, (size, size), 0)
    col_ids = lax.broadcasted_iota(jnp.int32, (size, size), 1)
    identity = (row_ids == col_ids).astype(jnp.float32)
    both = jnp.concatenate([block, identity], axis=1)
    tiles = [both[STEP * g : STEP * g + STEP] for g in range(size // STEP)]
    shape = tiles[0].shape
    lane = lax.broadcasted_iota(jnp.int32, shape, 0)
    pivots = [None] * len(tiles)
    for g in range(len(tiles)):
        later = range(g, len(tiles))
        start = STEP * g
        cols = [
            {h: jnp.broadcast_to(tiles[h][:, start + q : start + q + 1], shape) for h in later}
            for q in range(STEP)
        ]
        rows = [jnp.broadcast_to(tiles[g][a : a + 1], shape) for a in range(STEP)]
        piv = [
            [jnp.broadcast_to(cols[b][g][a : a + 1], shape) for b in range(a + 1)]
            for a in range(STEP)
        ]
        inverse = [None] * STEP
        for q in range(STEP):
            if q % 2 == 0:
                inverse[q] = 1.0 / piv[q][q]
                inverse[q + 1] = piv[q][q] / (
                    piv[q][q] * piv[q + 1][q + 1] - piv[q + 1][q] * piv[q + 1][q]
                )
            for a in range(q + 1, STEP):
                ratio = piv[a][q] * inverse[q]
                for b in range(q + 1, a + 1):
                    piv[a][b] = piv[a][b] - ratio * piv[b][q]
                rows[a] = rows[a] - ratio * rows[q]
                for h in later:
                    cols[a][h] = cols[a][h] - ratio * cols[q][h]
        pivots[g] = piv[0][0]
        for q in range(1, STEP):
            pivots[g] = jnp.where(lane == q, piv[q][q], pivots[g])
        for h in later:
            for q in range(STEP):
                if h == g and q == STEP - 1:
                    continue
                factor = cols[q][h] * inverse[q]
                if h == g:
                    factor = jnp.where(lane > q, factor, 0.0)
                tiles[h] = tiles[h] - factor * rows[q]
    done = [t[:, size:] * lax.rsqrt(p[:, size:]) for t, p in zip(tiles, pivots)]
    return jnp.concatenate(done, axis=0)


def factor_inverse(whole):
    count = whole.shape[0] // TILE
    left = [
        [whole[TILE * i : TILE * i + TILE, TILE * j : TILE * j + TILE] for j in range(count)]
        for i in range(count)
    ]
    lower = [[None] * count for _ in range(count)]
    inverse = [[jnp.zeros((TILE, TILE), jnp.float32)] * count for _ in range(count)]
    for k in range(count):
        inverse[k][k] = small_inverse(left[k][k])
        for i in range(k + 1, count):
            lower[i][k] = outer_rows(left[i][k], inverse[k][k])
        for i in range(k + 1, count):
            for j in range(k + 1, i + 1):
                left[i][j] = left[i][j] - outer_rows(lower[i][k], lower[j][k])
        for j in range(k):
            total = product(lower[k][j], inverse[j][j])
            for m in range(j + 1, k):
                total = total + product(lower[k][m], inverse[m][j])
            inverse[k][j] = -product(inverse[k][k], total)
    return jnp.concatenate([jnp.concatenate(row, axis=1) for row in inverse], axis=0)


def gathered_rows(parts):
    count = parts.shape[1] // TILE
    rows = []
    for g in range(count):
        rows.append(
            jnp.concatenate(
                [
                    parts[TILE * c : TILE * c + TILE, TILE * g : TILE * g + TILE]
                    for c in range(count)
                ],
                axis=1,
            )
        )
    return jnp.concatenate(rows, axis=0)


def finish_kernel(
    flags_ref,
    mine_ref,
    other_ref,
    embeddings_ref,
    parts_ref,
    first_ref,
    second_ref,
    points_ref,
    raw_ref,
    inverse_ref,
):
    size, width = embeddings_ref.shape
    half = mine_ref.shape[-1]
    split = width - half
    is_first = flags_ref[0] == 0

    def place(step, _):
        c, near = step // 4, step % 4
        for pair in range(2):
            row = pl.multiple_of(step * 16 + pair * 8, 8)
            for k in range(2):
                mine = [mine_ref[4 * c + 2 * pair + e, near] for e in range(2)]
                other = [other_ref[4 * c + 2 * pair + e, near] for e in range(2)]
                use_mine = is_first if k == 0 else jnp.logical_not(is_first)
                even, odd = [jnp.where(use_mine, m, o) for m, o in zip(mine, other)]
                for p in range(2):
                    rows = jnp.concatenate(
                        [even[4 * p : 4 * p + 4], odd[4 * p : 4 * p + 4]], axis=0
                    )
                    if k == 0:
                        points_ref[p, pl.ds(row, 8), :half] = rows
                    else:
                        points_ref[p, pl.ds(row, 8), half:] = rows[:, :split]
                        raw_ref[p, pl.ds(row, 8), :] = rows[:, split:]
        return 0

    lax.fori_loop(0, 16, place, 0)
    scale = -1.0 / (2.0 * width)
    row_ids = lax.broadcasted_iota(jnp.int32, (size, size), 0)
    col_ids = lax.broadcasted_iota(jnp.int32, (size, size), 1)
    ridge = jnp.where(row_ids == col_ids, ridge_weight, 0.0)
    points = [points_ref[p] for p in range(2)]
    knowns = [gathered_rows(raw_ref[p]) for p in range(2)]
    known = gathered_rows(parts_ref[...])
    embeddings = embeddings_ref[...]
    ones = jnp.ones((8, width), jnp.float32)
    col_norms = [outer_rows(ones, p * p)[:1] for p in points]
    norms = [jnp.sum(p * p, axis=1, keepdims=True) for p in points]
    row_norms = jnp.sum(embeddings * embeddings, axis=1, keepdims=True)

    def schur(rows, rows_norm, rows_known, panel):
        inner = outer_rows(rows, points[panel])
        kernel = jnp.exp((rows_norm + col_norms[panel] - 2.0 * inner) * scale)
        return kernel - outer_rows(rows_known, knowns[panel])

    top = schur(points[0], norms[0], knowns[0], 0) + ridge
    first = factor_inverse(top)
    inverse_ref[0] = first
    side = schur(points[1], norms[1], knowns[1], 0)
    low = schur(points[1], norms[1], knowns[1], 1) + ridge
    below = outer_rows(side, first)
    inverse_ref[1] = factor_inverse(low - outer_rows(below, below))
    first_rows = schur(embeddings, row_norms, known, 0)
    first_rows = first_rows + jnp.where(flags_ref[1] == 0, ridge, 0.0)
    second_rows = schur(embeddings, row_norms, known, 1)
    second_rows = second_rows + jnp.where(flags_ref[1] == 1, ridge, 0.0)
    first_panel = outer_rows(first_rows, first)
    second_rows = second_rows - outer_rows(first_panel, below)
    columns = first_ref.shape[1]
    own = pl.ds(pl.multiple_of(flags_ref[2] * columns, 8), columns)
    first_ref[...] = outer_rows(first_rows, inverse_ref[0, own, :])
    second = outer_rows(second_rows, inverse_ref[1, own, :])
    second_ref[...] = jnp.where(flags_ref[1] < 1, 0.0, second)


def finish(flags, mine, other, embeddings, parts):
    size, width = embeddings.shape
    known = parts.shape[1]
    columns = size // lax.axis_size("role")
    out = jax.ShapeDtypeStruct((size, columns), jnp.float32)
    whole = pl.BlockSpec(memory_space=pltpu.VMEM)
    return pl.pallas_call(
        finish_kernel,
        in_specs=[pl.BlockSpec(memory_space=pltpu.SMEM)] + [whole] * 4,
        out_specs=(whole, whole),
        out_shape=(out, out),
        scratch_shapes=[
            pltpu.VMEM((2, size, width), jnp.float32),
            pltpu.VMEM((2, size, known), jnp.float32),
            pltpu.VMEM((2, size, size), jnp.float32),
        ],
        name="finish",
    )(flags, mine, other, embeddings, parts)


def broadcast_panels(payload, known_wide, owners):
    far_count, near_count = lax.axis_size("far"), lax.axis_size("near")
    x_count, core_count = lax.axis_size("x"), lax.axis_size("core")
    rows, width = payload.shape
    groups = near_count * x_count
    high, half = rows // groups, width // core_count
    pieces = payload.reshape(groups, high, core_count, half)
    pieces = pieces.transpose(0, 2, 1, 3).reshape(groups * core_count, high, half)
    seen = exchange(pieces, ("near", "x", "core"))
    parts = copies_from(known_wide, "role")
    seen, parts = lax.optimization_barrier((seen, parts))
    sources, fars = [], []
    for owner in owners:
        core, place = owner % core_count, owner // core_count
        near, place = place % near_count, place // near_count
        far, x = place % far_count, place // far_count
        sources.append((near * x_count + x) * core_count + core)
        fars.append(far)
    own = jnp.concatenate([pick(seen, source) for source in sources], axis=0)
    seen = copies_from(own, ("far", "near"))
    seen = seen.reshape(far_count, near_count, len(owners) * high, half)
    strips = [pick(seen, far) for far in fars]
    sub = lax.broadcasted_iota(jnp.int32, strips[0].shape, 1)
    strip = jnp.where(sub < high, strips[0], strips[1])
    mine = copies_from(strip, ("role", "x"))
    other = lax.ppermute(mine, "core", [(0, 1), (1, 0)])
    return mine, other, parts


def on_device(embeddings, earlier_factor, block_of):
    size = embeddings.shape[0]
    role_count = lax.axis_size("role")
    columns = size // role_count
    role = lax.axis_index("role")
    slot = lax.axis_index(ROWS)
    my_block = lax.dynamic_index_in_dim(block_of, slot, 0, keepdims=False)
    slots = jnp.arange(block_of.shape[0], dtype=jnp.int32)
    owners = [jnp.sum(jnp.where(block_of == panel, slots, 0)) for panel in range(2)]

    own_points = lax.dynamic_slice_in_dim(embeddings, role * columns, columns, 0)
    known_wide = jnp.concatenate(
        [earlier_factor[g * columns : (g + 1) * columns] for g in range(role_count)], axis=1
    )
    payload = jnp.concatenate([own_points, known_wide], axis=1)
    mine, other, parts = broadcast_panels(payload, known_wide, owners)
    flags = jnp.stack([lax.axis_index("core"), my_block, role])
    parts = parts.reshape(size, -1)
    first_panel, second_panel = finish(flags, mine, other, embeddings, parts)
    return jnp.stack([first_panel, second_panel], axis=1)


def solution(mesh):
    finer = Mesh(
        mesh.devices.reshape(mesh.shape["role"], 4, 4, 4, 2), ("role", *ROWS)
    )
    placed = (P(ROWS, None), P(ROWS, "role"), P())
    return jax.shard_map(
        on_device, mesh=finer, in_specs=placed, out_specs=P(ROWS, None, "role"), check_vma=False
    )
```

```python
import jax
import jax.numpy as jnp
from jax import lax
from jax.experimental import pallas as pl
from jax.experimental.pallas import tpu as pltpu
from jax.sharding import Mesh
from jax.sharding import PartitionSpec as P

ROWS = ("x", "far", "near", "core")

highest = lax.Precision.HIGHEST
ridge_weight = 1.0
TILE = 64
STEP = 8


def outer_rows(rows, columns):
    return lax.dot_general(
        rows,
        columns,
        (((1,), (1,)), ((), ())),
        precision=highest,
        preferred_element_type=jnp.float32,
    )


def product(left, right):
    return lax.dot_general(
        left,
        right,
        (((1,), (0,)), ((), ())),
        precision=highest,
        preferred_element_type=jnp.float32,
    )


def exchange(array, axis):
    return lax.all_to_all(array, axis, 0, 0, tiled=True)


def copies_from(array, axis):
    count = lax.axis_size(axis)
    return exchange(jnp.broadcast_to(array[None], (count, *array.shape)), axis)


def pick(array, index):
    return lax.dynamic_index_in_dim(array, index, 0, keepdims=False)


def small_inverse(block):
    size = block.shape[0]
    row_ids = lax.broadcasted_iota(jnp.int32, (size, size), 0)
    col_ids = lax.broadcasted_iota(jnp.int32, (size, size), 1)
    identity = (row_ids == col_ids).astype(jnp.float32)
    both = jnp.concatenate([block, identity], axis=1)
    tiles = [both[STEP * g : STEP * g + STEP] for g in range(size // STEP)]
    shape = tiles[0].shape
    lane = lax.broadcasted_iota(jnp.int32, shape, 0)
    pivots = [None] * len(tiles)
    for g in range(len(tiles)):
        later = range(g, len(tiles))
        start = STEP * g
        cols = [
            {h: jnp.broadcast_to(tiles[h][:, start + q : start + q + 1], shape) for h in later}
            for q in range(STEP)
        ]
        rows = [jnp.broadcast_to(tiles[g][a : a + 1], shape) for a in range(STEP)]
        piv = [
            [jnp.broadcast_to(cols[b][g][a : a + 1], shape) for b in range(a + 1)]
            for a in range(STEP)
        ]
        inverse = [None] * STEP
        for q in range(STEP):
            if q % 2 == 0:
                inverse[q] = 1.0 / piv[q][q]
                inverse[q + 1] = piv[q][q] / (
                    piv[q][q] * piv[q + 1][q + 1] - piv[q + 1][q] * piv[q + 1][q]
                )
            for a in range(q + 1, STEP):
                ratio = piv[a][q] * inverse[q]
                for b in range(q + 1, a + 1):
                    piv[a][b] = piv[a][b] - ratio * piv[b][q]
                rows[a] = rows[a] - ratio * rows[q]
                for h in later:
                    cols[a][h] = cols[a][h] - ratio * cols[q][h]
        pivots[g] = piv[0][0]
        for q in range(1, STEP):
            pivots[g] = jnp.where(lane == q, piv[q][q], pivots[g])
        for h in later:
            terms = []
            for q in range(STEP - 1 if h == g else STEP):
                factor = cols[q][h] * inverse[q]
                if h == g:
                    factor = jnp.where(lane > q, factor, 0.0)
                terms.append(factor * rows[q])
            while len(terms) > 1:
                terms = [sum(terms[i : i + 2]) for i in range(0, len(terms), 2)]
            tiles[h] = tiles[h] - terms[0]
    done = [t[:, size:] * lax.rsqrt(p[:, size:]) for t, p in zip(tiles, pivots)]
    return jnp.concatenate(done, axis=0)


def factor_inverse(whole):
    count = whole.shape[0] // TILE
    left = [
        [whole[TILE * i : TILE * i + TILE, TILE * j : TILE * j + TILE] for j in range(count)]
        for i in range(count)
    ]
    lower = [[None] * count for _ in range(count)]
    inverse = [[jnp.zeros((TILE, TILE), jnp.float32)] * count for _ in range(count)]
    for k in range(count):
        inverse[k][k] = small_inverse(left[k][k])
        for i in range(k + 1, count):
            lower[i][k] = outer_rows(left[i][k], inverse[k][k])
        for i in range(k + 1, count):
            for j in range(k + 1, i + 1):
                left[i][j] = left[i][j] - outer_rows(lower[i][k], lower[j][k])
        for j in range(k):
            total = product(lower[k][j], inverse[j][j])
            for m in range(j + 1, k):
                total = total + product(lower[k][m], inverse[m][j])
            inverse[k][j] = -product(inverse[k][k], total)
    return jnp.concatenate([jnp.concatenate(row, axis=1) for row in inverse], axis=0)


def mesh_slot():
    slot = 0
    for axis in ROWS:
        slot = slot * lax.axis_size(axis) + lax.axis_index(axis)
    return slot


def finish_kernel(
    block_ref,
    mine_ref,
    other_ref,
    embeddings_ref,
    part_ref,
    near_ref,
    across_ref,
    back_ref,
    out_ref,
    points_ref,
    known_ref,
    inverse_ref,
):
    size, width = embeddings_ref.shape
    half = mine_ref.shape[-1]
    split = width - half
    columns = part_ref.shape[0]
    is_first = lax.axis_index("core") == 0
    role = lax.axis_index("role")
    my_block = block_ref[mesh_slot()]

    def place(step, _):
        c, near = step // 4, step % 4
        for pair in range(2):
            row = pl.multiple_of(step * 16 + pair * 8, 8)
            for k in range(2):
                mine = [mine_ref[4 * c + 2 * pair + e, near] for e in range(2)]
                other = [other_ref[4 * c + 2 * pair + e, near] for e in range(2)]
                use_mine = is_first if k == 0 else jnp.logical_not(is_first)
                even, odd = [jnp.where(use_mine, m, o) for m, o in zip(mine, other)]
                for p in range(2):
                    rows = jnp.concatenate(
                        [even[4 * p : 4 * p + 4], odd[4 * p : 4 * p + 4]], axis=0
                    )
                    if k == 0:
                        points_ref[p, pl.ds(row, 8), :half] = rows
                    else:
                        points_ref[p, pl.ds(row, 8), half:] = rows[:, :split]
                        known_ref[p, pl.ds(row, 8), :] = rows[:, split:]
        return 0

    lax.fori_loop(0, 16, place, 0)
    for step, ref in enumerate((part_ref, near_ref, across_ref, back_ref)):
        source = lax.rem(role + 4 - step, 4)
        known_ref[2, pl.ds(pl.multiple_of(source * columns, 8), columns), :] = ref[...]
    scale = -1.0 / (2.0 * width)
    row_ids = lax.broadcasted_iota(jnp.int32, (size, size), 0)
    col_ids = lax.broadcasted_iota(jnp.int32, (size, size), 1)
    ridge = jnp.where(row_ids == col_ids, ridge_weight, 0.0)
    points = [points_ref[p] for p in range(2)]
    knowns = [known_ref[p] for p in range(2)]
    embeddings = embeddings_ref[...]
    ones = jnp.ones((8, width), jnp.float32)
    col_norms = [outer_rows(ones, p * p)[:1] for p in points]
    norms = [jnp.sum(p * p, axis=1, keepdims=True) for p in points]
    row_norms = jnp.sum(embeddings * embeddings, axis=1, keepdims=True)

    def schur(rows, rows_norm, rows_known, panel):
        inner = outer_rows(rows, points[panel])
        kernel = jnp.exp((rows_norm + col_norms[panel] - 2.0 * inner) * scale)
        return kernel - product(rows_known, knowns[panel])

    first_known, second_known = knowns[0].T, knowns[1].T
    top = schur(points[0], norms[0], first_known, 0) + ridge
    first = factor_inverse(top)
    inverse_ref[0] = first
    side = schur(points[1], norms[1], second_known, 0)
    low = schur(points[1], norms[1], second_known, 1) + ridge
    below = outer_rows(side, first)
    inverse_ref[1] = factor_inverse(low - outer_rows(below, below))
    known = known_ref[2].T
    first_rows = schur(embeddings, row_norms, known, 0)
    first_rows = first_rows + jnp.where(my_block == 0, ridge, 0.0)
    second_rows = schur(embeddings, row_norms, known, 1)
    second_rows = second_rows + jnp.where(my_block == 1, ridge, 0.0)
    first_panel = outer_rows(first_rows, first)
    second_rows = second_rows - outer_rows(first_panel, below)
    own = pl.ds(pl.multiple_of(role * columns, 8), columns)
    out_ref[0] = outer_rows(inverse_ref[0, own, :], first_rows)
    second = outer_rows(inverse_ref[1, own, :], second_rows)
    out_ref[1] = jnp.where(my_block < 1, 0.0, second)


def finish(block_of, mine, other, embeddings, parts):
    size, width = embeddings.shape
    columns, known = parts[0].shape
    whole = pl.BlockSpec(memory_space=pltpu.VMEM)
    return pl.pallas_call(
        finish_kernel,
        in_specs=[pl.BlockSpec(memory_space=pltpu.SMEM)] + [whole] * 7,
        out_specs=whole,
        out_shape=jax.ShapeDtypeStruct((2, columns, size), jnp.float32),
        scratch_shapes=[
            pltpu.VMEM((2, size, width), jnp.float32),
            pltpu.VMEM((3, size, size), jnp.float32),
            pltpu.VMEM((2, size, size), jnp.float32),
        ],
        compiler_params=pltpu.CompilerParams(vmem_limit_bytes=24 * 2**20),
        name="finish",
    )(block_of, mine, other, embeddings, *parts)


def broadcast_panels(payload, known, block_of):
    far_count, near_count = lax.axis_size("far"), lax.axis_size("near")
    x_count, core_count = lax.axis_size("x"), lax.axis_size("core")
    role_count = lax.axis_size("role")
    rows, width = payload.shape
    groups = near_count * x_count
    high, half = rows // groups, width // core_count
    blocks = block_of.reshape(x_count, far_count, near_count, core_count)
    blocks = lax.dynamic_index_in_dim(blocks, lax.axis_index("far"), 1, keepdims=False)
    blocks = blocks.transpose(1, 0, 2).reshape(-1, 1, 1)
    pieces = payload.reshape(groups, high, core_count, half)
    pieces = pieces.transpose(0, 2, 1, 3).reshape(groups * core_count, high, half)
    seen = exchange(pieces, ("near", "x", "core"))
    own = jnp.concatenate(
        [jnp.sum(jnp.where(blocks == panel, seen, 0.0), axis=0) for panel in range(2)], axis=0
    )
    own, known = lax.optimization_barrier((own, known))
    parts = [known] + [
        lax.ppermute(known, "role", [(i, (i + step) % role_count) for i in range(role_count)])
        for step in range(1, role_count)
    ]
    seen = copies_from(own, ("far", "near"))
    strip = jnp.sum(seen.reshape(far_count, near_count, *own.shape), axis=0)
    strip, *parts = lax.optimization_barrier((strip, *parts))
    mine = copies_from(strip, ("role", "x"))
    other = lax.ppermute(mine, "core", [(0, 1), (1, 0)])
    return mine, other, parts


def on_device(embeddings, earlier_factor, block_of):
    columns = embeddings.shape[0] // lax.axis_size("role")
    role = lax.axis_index("role")
    own_points = lax.dynamic_slice_in_dim(embeddings, role * columns, columns, 0)
    known = earlier_factor.T
    payload = jnp.concatenate([own_points, known], axis=1)
    mine, other, parts = broadcast_panels(payload, known, block_of)
    return finish(block_of, mine, other, embeddings, parts).transpose(2, 0, 1)


def solution(mesh):
    finer = Mesh(
        mesh.devices.reshape(mesh.shape["role"], 4, 4, 4, 2), ("role", *ROWS)
    )
    placed = (P(ROWS, None), P(ROWS, "role"), P())
    return jax.shard_map(
        on_device, mesh=finer, in_specs=placed, out_specs=P(ROWS, None, "role"), check_vma=False
    )
```

```python
import jax
import jax.numpy as jnp
from jax import lax
from jax.experimental import pallas as pl
from jax.experimental.pallas import tpu as pltpu
from jax.sharding import Mesh
from jax.sharding import PartitionSpec as P

ROWS = ("x", "far", "near", "core")

highest = lax.Precision.HIGHEST
ridge_weight = 1.0
TILE = 128
STEP = 8
CHUNK = 256
EVERY = 3


def outer_rows(rows, columns):
    return lax.dot_general(
        rows,
        columns,
        (((1,), (1,)), ((), ())),
        precision=highest,
        preferred_element_type=jnp.float32,
    )


def product(left, right):
    return lax.dot_general(
        left,
        right,
        (((1,), (0,)), ((), ())),
        precision=highest,
        preferred_element_type=jnp.float32,
    )


def exchange(array, axis):
    return lax.all_to_all(array, axis, 0, 0, tiled=True)


def copies_from(array, axis):
    count = lax.axis_size(axis)
    return exchange(jnp.broadcast_to(array[None], (count, *array.shape)), axis)


def pick(array, index):
    return lax.dynamic_index_in_dim(array, index, 0, keepdims=False)


def small_inverse(block, beside):
    size = block.shape[0]
    tiles = [block[STEP * g : STEP * g + STEP] for g in range(size // STEP)]
    shape = tiles[0].shape
    sub = lax.broadcasted_iota(jnp.int32, shape, 0)
    lane = lax.broadcasted_iota(jnp.int32, shape, 1)
    done = []
    for g in range(len(tiles)):
        start = STEP * g
        later = range(g + 1, len(tiles))
        here = (lane >= start) & (lane < start + STEP)
        cols = [
            {
                h: jnp.broadcast_to(tiles[h][:, start + q : start + q + 1], shape)
                for h in range(g, len(tiles))
            }
            for q in range(STEP)
        ]
        own = jnp.where(here, (lane == start + sub).astype(jnp.float32), tiles[g])
        rows = [jnp.broadcast_to(own[a : a + 1], shape) for a in range(STEP)]
        piv = [
            [jnp.broadcast_to(cols[b][g][a : a + 1], shape) for b in range(a + 1)]
            for a in range(STEP)
        ]
        inverse = [None] * STEP
        ratio = [[None] * STEP for _ in range(STEP)]
        for q in range(STEP):
            if q % 2 == 0:
                inverse[q] = 1.0 / piv[q][q]
                inverse[q + 1] = piv[q][q] / (
                    piv[q][q] * piv[q + 1][q + 1] - piv[q + 1][q] * piv[q + 1][q]
                )
            for a in range(q + 1, STEP):
                ratio[a][q] = piv[a][q] * inverse[q]
                for b in range(q + 1, a + 1):
                    piv[a][b] = piv[a][b] - ratio[a][q] * piv[b][q]
                rows[a] = rows[a] - ratio[a][q] * rows[q]
                for h in later[:1]:
                    cols[a][h] = cols[a][h] - ratio[a][q] * cols[q][h]
        scale, final = inverse[0], rows[0]
        for q in range(1, STEP):
            scale = jnp.where(sub == q, inverse[q], scale)
            final = jnp.where(sub == q, rows[q], final)
        done.append(jnp.where(lane < start + STEP, final * jnp.sqrt(scale), 0.0))
        rows = [rows[q] * inverse[q] for q in range(STEP)]
        solved = list(rows)
        for a in range(STEP - 1, 0, -1):
            for b in range(a):
                solved[b] = solved[b] - ratio[a][b] * solved[a]
        for h in later:
            use = rows if h == g + 1 else solved
            terms = [cols[q][h] * use[q] for q in range(STEP)]
            while len(terms) > 1:
                terms = [terms[i] + terms[i + 1] for i in range(0, len(terms), 2)]
            tiles[h] = jnp.where(here, 0.0, tiles[h]) - terms[0]
        beside()
    return jnp.concatenate(done, axis=0)


def factor_inverse(whole, beside):
    count = whole.shape[0] // TILE
    left = [
        [whole[TILE * i : TILE * i + TILE, TILE * j : TILE * j + TILE] for j in range(count)]
        for i in range(count)
    ]
    lower = [[None] * count for _ in range(count)]
    inverse = [[jnp.zeros((TILE, TILE), jnp.float32)] * count for _ in range(count)]
    for k in range(count):
        inverse[k][k] = small_inverse(left[k][k], beside)
        for i in range(k + 1, count):
            lower[i][k] = outer_rows(left[i][k], inverse[k][k])
        for i in range(k + 1, count):
            for j in range(k + 1, i + 1):
                left[i][j] = left[i][j] - outer_rows(lower[i][k], lower[j][k])
        for j in range(k):
            total = product(lower[k][j], inverse[j][j])
            for m in range(j + 1, k):
                total = total + product(lower[k][m], inverse[m][j])
            inverse[k][j] = -product(inverse[k][k], total)
    return jnp.concatenate([jnp.concatenate(row, axis=1) for row in inverse], axis=0)


def mesh_slot():
    slot = 0
    for axis in ROWS:
        slot = slot * lax.axis_size(axis) + lax.axis_index(axis)
    return slot


def finish_kernel(
    block_ref,
    mine_ref,
    other_ref,
    embeddings_ref,
    part_ref,
    near_ref,
    across_ref,
    back_ref,
    out_ref,
    points_ref,
    known_ref,
    inverse_ref,
    turned_ref,
    rows_ref,
):
    size, width = embeddings_ref.shape
    half = mine_ref.shape[-1]
    split = width - half
    columns = part_ref.shape[0]
    is_first = lax.axis_index("core") == 0
    role = lax.axis_index("role")
    my_block = block_ref[mesh_slot()]

    def place(step, _):
        c, near = step // 4, step % 4
        for pair in range(2):
            row = pl.multiple_of(step * 16 + pair * 8, 8)
            for k in range(2):
                mine = [mine_ref[4 * c + 2 * pair + e, near] for e in range(2)]
                other = [other_ref[4 * c + 2 * pair + e, near] for e in range(2)]
                use_mine = is_first if k == 0 else jnp.logical_not(is_first)
                even, odd = [jnp.where(use_mine, m, o) for m, o in zip(mine, other)]
                for p in range(2):
                    rows = jnp.concatenate(
                        [even[4 * p : 4 * p + 4], odd[4 * p : 4 * p + 4]], axis=0
                    )
                    if k == 0:
                        points_ref[p, pl.ds(row, 8), :half] = rows
                    else:
                        points_ref[p, pl.ds(row, 8), half:] = rows[:, :split]
                        known_ref[p, pl.ds(row, 8), :] = rows[:, split:]
        return 0

    lax.fori_loop(0, 16, place, 0)
    for step, ref in enumerate((part_ref, near_ref, across_ref, back_ref)):
        source = lax.rem(role + 4 - step, 4)
        known_ref[2, pl.ds(pl.multiple_of(source * columns, 8), columns), :] = ref[...]
    scale = -1.0 / (2.0 * width)
    row_ids = lax.broadcasted_iota(jnp.int32, (size, size), 0)
    col_ids = lax.broadcasted_iota(jnp.int32, (size, size), 1)
    ridge = jnp.where(row_ids == col_ids, ridge_weight, 0.0)
    ones = jnp.ones((8, width), jnp.float32)
    col_norms = [outer_rows(ones, points_ref[p] * points_ref[p])[:1] for p in range(2)]
    turned_ref[0] = known_ref[0].T

    def schur(row_ref, panel, turned, start, count):
        chunk = pl.ds(start, count)
        rows = row_ref[chunk, :]
        norms = jnp.sum(rows * rows, axis=1, keepdims=True)
        inner = outer_rows(rows, points_ref[panel])
        kernel = jnp.exp((norms + col_norms[panel] - 2.0 * inner) * scale)
        return kernel - product(turned_ref[turned, chunk, :], known_ref[panel])

    def schur_piece(target, row_ref, panel, turned, start):
        def emit():
            rows_ref[target, pl.ds(start, CHUNK), :] = schur(row_ref, panel, turned, start, CHUNK)

        return emit

    def turn(index):
        def emit():
            turned_ref[index] = known_ref[index].T

        return emit

    def spread(work):
        count, state = len(work), [0, 0]

        def beside():
            state[0] += 1
            if state[0] % EVERY == 0 and state[1] < count:
                work[state[1]]()
                state[1] += 1

        def rest():
            while state[1] < count:
                work[state[1]]()
                state[1] += 1

        return beside, rest

    starts = range(0, size, CHUNK)
    jobs = [(0, points_ref.at[1], 0, 1), (1, points_ref.at[1], 1, 1)]
    jobs += [(2, embeddings_ref, 0, 2), (3, embeddings_ref, 1, 2)]
    work = [turn(1), turn(2)]
    work += [schur_piece(*job, start) for job in jobs for start in starts]
    beside, rest = spread(work)
    first = factor_inverse(schur(points_ref.at[0], 0, 0, 0, size) + ridge, beside)
    rest()
    inverse_ref[0] = first
    below = outer_rows(rows_ref[0], first)
    own = pl.ds(pl.multiple_of(role * columns, 8), columns)
    first_rows = rows_ref[2] + jnp.where(my_block == 0, ridge, 0.0)

    def panel_piece(start):
        def emit():
            chunk = slice(start, start + CHUNK)
            panel = outer_rows(first_rows[chunk], first)
            second_rows = rows_ref[3, pl.ds(start, CHUNK), :] - outer_rows(panel, below)
            here = jnp.where(my_block == 1, ridge[chunk], 0.0)
            rows_ref[3, pl.ds(start, CHUNK), :] = second_rows + here

        return emit

    def first_output():
        out_ref[0] = outer_rows(inverse_ref[0, own, :], first_rows)

    beside, rest = spread([panel_piece(start) for start in starts] + [first_output])
    inverse_ref[1] = factor_inverse(rows_ref[1] + ridge - outer_rows(below, below), beside)
    rest()
    second = outer_rows(inverse_ref[1, own, :], rows_ref[3])
    out_ref[1] = jnp.where(my_block < 1, 0.0, second)


def finish(block_of, mine, other, embeddings, parts):
    size, width = embeddings.shape
    columns, known = parts[0].shape
    whole = pl.BlockSpec(memory_space=pltpu.VMEM)
    return pl.pallas_call(
        finish_kernel,
        in_specs=[pl.BlockSpec(memory_space=pltpu.SMEM)] + [whole] * 7,
        out_specs=whole,
        out_shape=jax.ShapeDtypeStruct((2, columns, size), jnp.float32),
        scratch_shapes=[
            pltpu.VMEM((2, size, width), jnp.float32),
            pltpu.VMEM((3, size, size), jnp.float32),
            pltpu.VMEM((2, size, size), jnp.float32),
            pltpu.VMEM((3, size, size), jnp.float32),
            pltpu.VMEM((4, size, size), jnp.float32),
        ],
        compiler_params=pltpu.CompilerParams(vmem_limit_bytes=24 * 2**20),
        name="finish",
    )(block_of, mine, other, embeddings, *parts)


def broadcast_panels(payload, known, block_of):
    far_count, near_count = lax.axis_size("far"), lax.axis_size("near")
    x_count, core_count = lax.axis_size("x"), lax.axis_size("core")
    role_count = lax.axis_size("role")
    rows, width = payload.shape
    groups = near_count * x_count
    high, half = rows // groups, width // core_count
    blocks = block_of.reshape(x_count, far_count, near_count, core_count)
    blocks = lax.dynamic_index_in_dim(blocks, lax.axis_index("far"), 1, keepdims=False)
    blocks = blocks.transpose(1, 0, 2).reshape(-1, 1, 1)
    pieces = payload.reshape(groups, high, core_count, half)
    pieces = pieces.transpose(0, 2, 1, 3).reshape(groups * core_count, high, half)
    seen = exchange(pieces, ("near", "x", "core"))
    own = jnp.concatenate(
        [jnp.sum(jnp.where(blocks == panel, seen, 0.0), axis=0) for panel in range(2)], axis=0
    )
    parts = [known] + [
        lax.ppermute(known, "role", [(i, (i + step) % role_count) for i in range(role_count)])
        for step in range(1, role_count)
    ]
    own, *parts = lax.optimization_barrier((own, *parts))
    seen = copies_from(own, ("far", "near"))
    strip = jnp.sum(seen.reshape(far_count, near_count, *own.shape), axis=0)
    mine = copies_from(strip, ("role", "x"))
    other = lax.ppermute(mine, "core", [(0, 1), (1, 0)])
    return mine, other, parts


def on_device(embeddings, earlier_factor, block_of):
    columns = embeddings.shape[0] // lax.axis_size("role")
    role = lax.axis_index("role")
    own_points = lax.dynamic_slice_in_dim(embeddings, role * columns, columns, 0)
    known = earlier_factor.T
    payload = jnp.concatenate([own_points, known], axis=1)
    mine, other, parts = broadcast_panels(payload, known, block_of)
    return finish(block_of, mine, other, embeddings, parts).transpose(2, 0, 1)


def solution(mesh):
    finer = Mesh(
        mesh.devices.reshape(mesh.shape["role"], 4, 4, 4, 2), ("role", *ROWS)
    )
    placed = (P(ROWS, None), P(ROWS, "role"), P())
    return jax.shard_map(
        on_device, mesh=finer, in_specs=placed, out_specs=P(ROWS, None, "role"), check_vma=False
    )
```

```python
import jax
import jax.numpy as jnp
from jax import lax
from jax.experimental import pallas as pl
from jax.experimental.pallas import tpu as pltpu
from jax.sharding import Mesh
from jax.sharding import PartitionSpec as P

ROWS = ("x", "far", "near", "core")

highest = lax.Precision.HIGHEST
ridge_weight = 1.0
TILE = 128
STEP = 8
CHUNK = 256
EVERY = 3


def outer_rows(rows, columns):
    return lax.dot_general(
        rows,
        columns,
        (((1,), (1,)), ((), ())),
        precision=highest,
        preferred_element_type=jnp.float32,
    )


def product(left, right):
    return lax.dot_general(
        left,
        right,
        (((1,), (0,)), ((), ())),
        precision=highest,
        preferred_element_type=jnp.float32,
    )


def exchange(array, axis):
    return lax.all_to_all(array, axis, 0, 0, tiled=True)


def copies_from(array, axis):
    count = lax.axis_size(axis)
    return exchange(jnp.broadcast_to(array[None], (count, *array.shape)), axis)


def pick(array, index):
    return lax.dynamic_index_in_dim(array, index, 0, keepdims=False)


def small_inverse(block, beside):
    size = block.shape[0]
    tiles = [block[STEP * g : STEP * g + STEP] for g in range(size // STEP)]
    shape = tiles[0].shape
    sub = lax.broadcasted_iota(jnp.int32, shape, 0)
    lane = lax.broadcasted_iota(jnp.int32, shape, 1)
    done = []
    for g in range(len(tiles)):
        start = STEP * g
        later = range(g + 1, len(tiles))
        here = (lane >= start) & (lane < start + STEP)
        cols = [
            {
                h: jnp.broadcast_to(tiles[h][:, start + q : start + q + 1], shape)
                for h in range(g, len(tiles))
            }
            for q in range(STEP)
        ]
        own = jnp.where(here, (lane == start + sub).astype(jnp.float32), tiles[g])
        rows = [jnp.broadcast_to(own[a : a + 1], shape) for a in range(STEP)]
        piv = [
            [jnp.broadcast_to(cols[b][g][a : a + 1], shape) for b in range(a + 1)]
            for a in range(STEP)
        ]
        inverse = [None] * STEP
        ratio = [[None] * STEP for _ in range(STEP)]
        for q in range(STEP):
            if q % 2 == 0:
                inverse[q] = 1.0 / piv[q][q]
                inverse[q + 1] = piv[q][q] / (
                    piv[q][q] * piv[q + 1][q + 1] - piv[q + 1][q] * piv[q + 1][q]
                )
            for a in range(q + 1, STEP):
                ratio[a][q] = piv[a][q] * inverse[q]
                for b in range(q + 1, a + 1):
                    piv[a][b] = piv[a][b] - ratio[a][q] * piv[b][q]
                rows[a] = rows[a] - ratio[a][q] * rows[q]
                for h in later[:1]:
                    cols[a][h] = cols[a][h] - ratio[a][q] * cols[q][h]
        scale, final = inverse[0], rows[0]
        for q in range(1, STEP):
            scale = jnp.where(sub == q, inverse[q], scale)
            final = jnp.where(sub == q, rows[q], final)
        done.append(jnp.where(lane < start + STEP, final * jnp.sqrt(scale), 0.0))
        rows = [rows[q] * inverse[q] for q in range(STEP)]
        solved = list(rows)
        for a in range(STEP - 1, 0, -1):
            for b in range(a):
                solved[b] = solved[b] - ratio[a][b] * solved[a]
        for h in later:
            use = rows if h == g + 1 else solved
            terms = [cols[q][h] * use[q] for q in range(STEP)]
            while len(terms) > 1:
                terms = [terms[i] + terms[i + 1] for i in range(0, len(terms), 2)]
            tiles[h] = jnp.where(here, 0.0, tiles[h]) - terms[0]
        beside()
    return jnp.concatenate(done, axis=0)


def factor_inverse(whole, beside):
    count = whole.shape[0] // TILE
    left = [
        [whole[TILE * i : TILE * i + TILE, TILE * j : TILE * j + TILE] for j in range(count)]
        for i in range(count)
    ]
    lower = [[None] * count for _ in range(count)]
    inverse = [[jnp.zeros((TILE, TILE), jnp.float32)] * count for _ in range(count)]
    for k in range(count):
        inverse[k][k] = small_inverse(left[k][k], beside)
        for i in range(k + 1, count):
            lower[i][k] = outer_rows(left[i][k], inverse[k][k])
        for i in range(k + 1, count):
            for j in range(k + 1, i + 1):
                left[i][j] = left[i][j] - outer_rows(lower[i][k], lower[j][k])
        for j in range(k):
            total = product(lower[k][j], inverse[j][j])
            for m in range(j + 1, k):
                total = total + product(lower[k][m], inverse[m][j])
            inverse[k][j] = -product(inverse[k][k], total)
    return jnp.concatenate([jnp.concatenate(row, axis=1) for row in inverse], axis=0)


def mesh_slot():
    slot = 0
    for axis in ROWS:
        slot = slot * lax.axis_size(axis) + lax.axis_index(axis)
    return slot


def finish_kernel(
    block_ref,
    mine_ref,
    other_ref,
    embeddings_ref,
    part_ref,
    near_ref,
    across_ref,
    back_ref,
    out_ref,
    points_ref,
    known_ref,
    inverse_ref,
    turned_ref,
    rows_ref,
):
    size, width = embeddings_ref.shape
    half = mine_ref.shape[-1]
    split = width - half
    columns = part_ref.shape[0]
    is_first = lax.axis_index("core") == 0
    role = lax.axis_index("role")
    my_block = block_ref[mesh_slot()]

    def place(step, _):
        c, near = step // 4, step % 4
        for pair in range(2):
            row = pl.multiple_of(step * 16 + pair * 8, 8)
            for k in range(2):
                mine = [mine_ref[4 * c + 2 * pair + e, near] for e in range(2)]
                other = [other_ref[4 * c + 2 * pair + e, near] for e in range(2)]
                use_mine = is_first if k == 0 else jnp.logical_not(is_first)
                even, odd = [jnp.where(use_mine, m, o) for m, o in zip(mine, other)]
                for p in range(2):
                    rows = jnp.concatenate(
                        [even[4 * p : 4 * p + 4], odd[4 * p : 4 * p + 4]], axis=0
                    )
                    if k == 0:
                        points_ref[p, pl.ds(row, 8), :half] = rows
                    else:
                        points_ref[p, pl.ds(row, 8), half:] = rows[:, :split]
                        known_ref[p, pl.ds(row, 8), :] = rows[:, split:]
        return 0

    lax.fori_loop(0, 16, place, 0)
    for step, ref in enumerate((part_ref, near_ref, across_ref, back_ref)):
        source = lax.rem(role + 4 - step, 4)
        known_ref[2, pl.ds(pl.multiple_of(source * columns, 8), columns), :] = ref[...]
    scale = -1.0 / (2.0 * width)
    row_ids = lax.broadcasted_iota(jnp.int32, (size, size), 0)
    col_ids = lax.broadcasted_iota(jnp.int32, (size, size), 1)
    ridge = jnp.where(row_ids == col_ids, ridge_weight, 0.0)
    ones = jnp.ones((8, width), jnp.float32)
    col_norms = [outer_rows(ones, points_ref[p] * points_ref[p])[:1] for p in range(2)]
    turned_ref[0] = known_ref[0].T

    def schur(row_ref, panel, turned, start, count):
        chunk = pl.ds(start, count)
        rows = row_ref[chunk, :]
        norms = jnp.sum(rows * rows, axis=1, keepdims=True)
        inner = outer_rows(rows, points_ref[panel])
        kernel = jnp.exp((norms + col_norms[panel] - 2.0 * inner) * scale)
        return kernel - product(turned_ref[turned, chunk, :], known_ref[panel])

    def schur_piece(target, row_ref, panel, turned, start):
        def emit():
            rows_ref[target, pl.ds(start, CHUNK), :] = schur(row_ref, panel, turned, start, CHUNK)

        return emit

    def turn(index):
        def emit():
            turned_ref[index] = known_ref[index].T

        return emit

    def spread(work):
        count, state = len(work), [0, 0]

        def beside():
            state[0] += 1
            if state[0] % EVERY == 0 and state[1] < count:
                work[state[1]]()
                state[1] += 1

        def rest():
            while state[1] < count:
                work[state[1]]()
                state[1] += 1

        return beside, rest

    starts = range(0, size, CHUNK)
    jobs = [(0, points_ref.at[1], 0, 1), (1, points_ref.at[1], 1, 1)]
    jobs += [(2, embeddings_ref, 0, 2), (3, embeddings_ref, 1, 2)]
    work = [turn(1), turn(2)]
    work += [schur_piece(*job, start) for job in jobs for start in starts]
    beside, rest = spread(work)
    first = factor_inverse(schur(points_ref.at[0], 0, 0, 0, size) + ridge, beside)
    rest()
    inverse_ref[0] = first
    below = outer_rows(rows_ref[0], first)
    own = pl.ds(pl.multiple_of(role * columns, 8), columns)
    first_rows = rows_ref[2] + jnp.where(my_block == 0, ridge, 0.0)

    def panel_piece(start):
        def emit():
            chunk = slice(start, start + CHUNK)
            panel = outer_rows(first_rows[chunk], first)
            second_rows = rows_ref[3, pl.ds(start, CHUNK), :] - outer_rows(panel, below)
            here = jnp.where(my_block == 1, ridge[chunk], 0.0)
            rows_ref[3, pl.ds(start, CHUNK), :] = second_rows + here

        return emit

    def first_output():
        out_ref[0] = outer_rows(inverse_ref[0, own, :], first_rows)

    beside, rest = spread([panel_piece(start) for start in starts] + [first_output])
    inverse_ref[1] = factor_inverse(rows_ref[1] + ridge - outer_rows(below, below), beside)
    rest()
    second = outer_rows(inverse_ref[1, own, :], rows_ref[3])
    out_ref[1] = jnp.where(my_block < 1, 0.0, second)


def finish(block_of, mine, other, embeddings, parts):
    size, width = embeddings.shape
    columns, known = parts[0].shape
    whole = pl.BlockSpec(memory_space=pltpu.VMEM)
    return pl.pallas_call(
        finish_kernel,
        in_specs=[pl.BlockSpec(memory_space=pltpu.SMEM)] + [whole] * 7,
        out_specs=whole,
        out_shape=jax.ShapeDtypeStruct((2, columns, size), jnp.float32),
        scratch_shapes=[
            pltpu.VMEM((2, size, width), jnp.float32),
            pltpu.VMEM((3, size, size), jnp.float32),
            pltpu.VMEM((2, size, size), jnp.float32),
            pltpu.VMEM((3, size, size), jnp.float32),
            pltpu.VMEM((4, size, size), jnp.float32),
        ],
        compiler_params=pltpu.CompilerParams(vmem_limit_bytes=24 * 2**20),
        name="finish",
    )(block_of, mine, other, embeddings, *parts)


def broadcast_panels(payload, known, block_of):
    far_count, near_count = lax.axis_size("far"), lax.axis_size("near")
    x_count, core_count = lax.axis_size("x"), lax.axis_size("core")
    role_count = lax.axis_size("role")
    rows, width = payload.shape
    groups = near_count * x_count
    high, half = rows // groups, width // core_count
    blocks = block_of.reshape(x_count, far_count, near_count, core_count)
    holds = [jnp.any(blocks == panel, axis=(0, 2, 3)) for panel in range(2)]
    apart = jnp.logical_not(jnp.any(holds[0] & holds[1]))
    blocks = lax.dynamic_index_in_dim(blocks, lax.axis_index("far"), 1, keepdims=False)
    blocks = blocks.transpose(1, 0, 2).reshape(-1, 1, 1)
    pieces = payload.reshape(groups, high, core_count, half)
    pieces = pieces.transpose(0, 2, 1, 3).reshape(groups * core_count, high, half)
    seen = exchange(pieces, ("near", "x", "core"))
    own = jnp.concatenate(
        [jnp.sum(jnp.where(blocks == panel, seen, 0.0), axis=0) for panel in range(2)], axis=0
    )
    parts = [known] + [
        lax.ppermute(known, "role", [(i, (i + step) % role_count) for i in range(role_count)])
        for step in range(1, role_count)
    ]
    own, *parts = lax.optimization_barrier((own, *parts))

    def gathered(strip):
        seen = copies_from(strip, ("far", "near"))
        return seen.reshape(far_count, near_count, *strip.shape)

    def whole_strips(own):
        return jnp.sum(gathered(own), axis=0)

    def half_strips(own):
        seen = gathered(own[:high] + own[high:])
        chosen = [
            jnp.sum(jnp.where(held.reshape(-1, 1, 1, 1), seen, 0.0), axis=0) for held in holds
        ]
        return jnp.concatenate(chosen, axis=1)

    strip = lax.cond(apart, half_strips, whole_strips, own)
    mine = copies_from(strip, ("role", "x"))
    other = lax.ppermute(mine, "core", [(0, 1), (1, 0)])
    return mine, other, parts


def on_device(embeddings, earlier_factor, block_of):
    columns = embeddings.shape[0] // lax.axis_size("role")
    role = lax.axis_index("role")
    own_points = lax.dynamic_slice_in_dim(embeddings, role * columns, columns, 0)
    known = earlier_factor.T
    payload = jnp.concatenate([own_points, known], axis=1)
    mine, other, parts = broadcast_panels(payload, known, block_of)
    return finish(block_of, mine, other, embeddings, parts).transpose(2, 0, 1)


def solution(mesh):
    finer = Mesh(
        mesh.devices.reshape(mesh.shape["role"], 4, 4, 4, 2), ("role", *ROWS)
    )
    placed = (P(ROWS, None), P(ROWS, "role"), P())
    return jax.shard_map(
        on_device, mesh=finer, in_specs=placed, out_specs=P(ROWS, None, "role"), check_vma=False
    )
```

```python
import jax
import jax.numpy as jnp
from jax import lax
from jax.experimental import pallas as pl
from jax.experimental.pallas import tpu as pltpu
from jax.sharding import Mesh
from jax.sharding import PartitionSpec as P

ROWS = ("x", "far", "near", "core")

highest = lax.Precision.HIGHEST
ridge_weight = 1.0
TILE = 128
STEP = 8
CHUNK = 256
EVERY = 3


def outer_rows(rows, columns):
    return lax.dot_general(
        rows,
        columns,
        (((1,), (1,)), ((), ())),
        precision=highest,
        preferred_element_type=jnp.float32,
    )


def product(left, right):
    return lax.dot_general(
        left,
        right,
        (((1,), (0,)), ((), ())),
        precision=highest,
        preferred_element_type=jnp.float32,
    )


def exchange(array, axis):
    return lax.all_to_all(array, axis, 0, 0, tiled=True)


def copies_from(array, axis):
    count = lax.axis_size(axis)
    return exchange(jnp.broadcast_to(array[None], (count, *array.shape)), axis)


def pick(array, index):
    return lax.dynamic_index_in_dim(array, index, 0, keepdims=False)


def small_inverse(block, beside):
    size = block.shape[0]
    tiles = [block[STEP * g : STEP * g + STEP] for g in range(size // STEP)]
    shape = tiles[0].shape
    sub = lax.broadcasted_iota(jnp.int32, shape, 0)
    lane = lax.broadcasted_iota(jnp.int32, shape, 1)
    done = []
    for g in range(len(tiles)):
        start = STEP * g
        later = range(g + 1, len(tiles))
        here = (lane >= start) & (lane < start + STEP)
        cols = [
            {
                h: jnp.broadcast_to(tiles[h][:, start + q : start + q + 1], shape)
                for h in range(g, len(tiles))
            }
            for q in range(STEP)
        ]
        own = jnp.where(here, (lane == start + sub).astype(jnp.float32), tiles[g])
        rows = [jnp.broadcast_to(own[a : a + 1], shape) for a in range(STEP)]
        piv = [
            [jnp.broadcast_to(cols[b][g][a : a + 1], shape) for b in range(a + 1)]
            for a in range(STEP)
        ]
        inverse = [None] * STEP
        ratio = [[None] * STEP for _ in range(STEP)]
        for q in range(STEP):
            if q % 2 == 0:
                inverse[q] = 1.0 / piv[q][q]
                inverse[q + 1] = piv[q][q] / (
                    piv[q][q] * piv[q + 1][q + 1] - piv[q + 1][q] * piv[q + 1][q]
                )
            for a in range(q + 1, STEP):
                ratio[a][q] = piv[a][q] * inverse[q]
                for b in range(q + 1, a + 1):
                    piv[a][b] = piv[a][b] - ratio[a][q] * piv[b][q]
                rows[a] = rows[a] - ratio[a][q] * rows[q]
                for h in later[:1]:
                    cols[a][h] = cols[a][h] - ratio[a][q] * cols[q][h]
        scale, final = inverse[0], rows[0]
        for q in range(1, STEP):
            scale = jnp.where(sub == q, inverse[q], scale)
            final = jnp.where(sub == q, rows[q], final)
        done.append(jnp.where(lane < start + STEP, final * jnp.sqrt(scale), 0.0))
        rows = [rows[q] * inverse[q] for q in range(STEP)]
        solved = list(rows)
        for a in range(STEP - 1, 0, -1):
            for b in range(a):
                solved[b] = solved[b] - ratio[a][b] * solved[a]
        for h in later:
            use = rows if h == g + 1 else solved
            terms = [cols[q][h] * use[q] for q in range(STEP)]
            while len(terms) > 1:
                terms = [terms[i] + terms[i + 1] for i in range(0, len(terms), 2)]
            tiles[h] = jnp.where(here, 0.0, tiles[h]) - terms[0]
        beside()
    return jnp.concatenate(done, axis=0)


def factor_inverse(whole, beside):
    count = whole.shape[0] // TILE
    left = [
        [whole[TILE * i : TILE * i + TILE, TILE * j : TILE * j + TILE] for j in range(count)]
        for i in range(count)
    ]
    lower = [[None] * count for _ in range(count)]
    inverse = [[jnp.zeros((TILE, TILE), jnp.float32)] * count for _ in range(count)]
    for k in range(count):
        inverse[k][k] = small_inverse(left[k][k], beside)
        for i in range(k + 1, count):
            lower[i][k] = outer_rows(left[i][k], inverse[k][k])
        for i in range(k + 1, count):
            for j in range(k + 1, i + 1):
                left[i][j] = left[i][j] - outer_rows(lower[i][k], lower[j][k])
        for j in range(k):
            total = product(lower[k][j], inverse[j][j])
            for m in range(j + 1, k):
                total = total + product(lower[k][m], inverse[m][j])
            inverse[k][j] = -product(inverse[k][k], total)
    return jnp.concatenate([jnp.concatenate(row, axis=1) for row in inverse], axis=0)


def mesh_slot():
    slot = 0
    for axis in ROWS:
        slot = slot * lax.axis_size(axis) + lax.axis_index(axis)
    return slot


def finish_kernel(
    block_ref,
    mine_ref,
    other_ref,
    embeddings_ref,
    part_ref,
    near_ref,
    across_ref,
    back_ref,
    out_ref,
    points_ref,
    known_ref,
    inverse_ref,
    turned_ref,
    rows_ref,
):
    size, width = embeddings_ref.shape
    half = mine_ref.shape[-1]
    split = width - half
    columns = part_ref.shape[0]
    is_first = lax.axis_index("core") == 0
    role = lax.axis_index("role")
    my_block = block_ref[mesh_slot()]

    def place(step, _):
        c, near = step // 4, step % 4
        for pair in range(2):
            row = pl.multiple_of(step * 16 + pair * 8, 8)
            for k in range(2):
                mine = [mine_ref[4 * c + 2 * pair + e, near] for e in range(2)]
                other = [other_ref[4 * c + 2 * pair + e, near] for e in range(2)]
                use_mine = is_first if k == 0 else jnp.logical_not(is_first)
                even, odd = [jnp.where(use_mine, m, o) for m, o in zip(mine, other)]
                for p in range(2):
                    rows = jnp.concatenate(
                        [even[4 * p : 4 * p + 4], odd[4 * p : 4 * p + 4]], axis=0
                    )
                    if k == 0:
                        points_ref[p, pl.ds(row, 8), :half] = rows
                    else:
                        points_ref[p, pl.ds(row, 8), half:] = rows[:, :split]
                        known_ref[p, pl.ds(row, 8), :] = rows[:, split:]
        return 0

    lax.fori_loop(0, 16, place, 0)
    for step, ref in enumerate((part_ref, near_ref, across_ref, back_ref)):
        source = lax.rem(role + 4 - step, 4)
        known_ref[2, pl.ds(pl.multiple_of(source * columns, 8), columns), :] = ref[...]
    scale = -1.0 / (2.0 * width)
    row_ids = lax.broadcasted_iota(jnp.int32, (size, size), 0)
    col_ids = lax.broadcasted_iota(jnp.int32, (size, size), 1)
    ridge = jnp.where(row_ids == col_ids, ridge_weight, 0.0)
    ones = jnp.ones((8, width), jnp.float32)
    col_norms = [outer_rows(ones, points_ref[p] * points_ref[p])[:1] for p in range(2)]
    turned_ref[0] = known_ref[0].T

    def schur(row_ref, panel, turned, start, count):
        chunk = pl.ds(start, count)
        rows = row_ref[chunk, :]
        norms = jnp.sum(rows * rows, axis=1, keepdims=True)
        inner = outer_rows(rows, points_ref[panel])
        kernel = jnp.exp((norms + col_norms[panel] - 2.0 * inner) * scale)
        return kernel - product(turned_ref[turned, chunk, :], known_ref[panel])

    def schur_piece(target, row_ref, panel, turned, start):
        def emit():
            rows_ref[target, pl.ds(start, CHUNK), :] = schur(row_ref, panel, turned, start, CHUNK)

        return emit

    def turn(index):
        def emit():
            turned_ref[index] = known_ref[index].T

        return emit

    def spread(work):
        count, state = len(work), [0, 0]

        def beside():
            state[0] += 1
            if state[0] % EVERY == 0 and state[1] < count:
                work[state[1]]()
                state[1] += 1

        def rest():
            while state[1] < count:
                work[state[1]]()
                state[1] += 1

        return beside, rest

    starts = range(0, size, CHUNK)
    jobs = [(0, points_ref.at[1], 0, 1), (1, points_ref.at[1], 1, 1)]
    jobs += [(2, embeddings_ref, 0, 2), (3, embeddings_ref, 1, 2)]
    work = [turn(1), turn(2)]
    work += [schur_piece(*job, start) for job in jobs for start in starts]
    beside, rest = spread(work)
    first = factor_inverse(schur(points_ref.at[0], 0, 0, 0, size) + ridge, beside)
    rest()
    inverse_ref[0] = first
    below = outer_rows(rows_ref[0], first)
    own = pl.ds(pl.multiple_of(role * columns, 8), columns)
    first_rows = rows_ref[2] + jnp.where(my_block == 0, ridge, 0.0)

    def panel_piece(start):
        def emit():
            chunk = slice(start, start + CHUNK)
            panel = outer_rows(first_rows[chunk], first)
            second_rows = rows_ref[3, pl.ds(start, CHUNK), :] - outer_rows(panel, below)
            here = jnp.where(my_block == 1, ridge[chunk], 0.0)
            rows_ref[3, pl.ds(start, CHUNK), :] = second_rows + here

        return emit

    def first_output():
        out_ref[0] = outer_rows(inverse_ref[0, own, :], first_rows)

    beside, rest = spread([panel_piece(start) for start in starts] + [first_output])
    inverse_ref[1] = factor_inverse(rows_ref[1] + ridge - outer_rows(below, below), beside)
    rest()
    second = outer_rows(inverse_ref[1, own, :], rows_ref[3])
    out_ref[1] = jnp.where(my_block < 1, 0.0, second)


def finish(block_of, mine, other, embeddings, parts):
    size, width = embeddings.shape
    columns, known = parts[0].shape
    whole = pl.BlockSpec(memory_space=pltpu.VMEM)
    return pl.pallas_call(
        finish_kernel,
        in_specs=[pl.BlockSpec(memory_space=pltpu.SMEM)] + [whole] * 7,
        out_specs=whole,
        out_shape=jax.ShapeDtypeStruct((2, columns, size), jnp.float32),
        scratch_shapes=[
            pltpu.VMEM((2, size, width), jnp.float32),
            pltpu.VMEM((3, size, size), jnp.float32),
            pltpu.VMEM((2, size, size), jnp.float32),
            pltpu.VMEM((3, size, size), jnp.float32),
            pltpu.VMEM((4, size, size), jnp.float32),
        ],
        compiler_params=pltpu.CompilerParams(vmem_limit_bytes=24 * 2**20),
        name="finish",
    )(block_of, mine, other, embeddings, *parts)


def broadcast_panels(payload, known, block_of):
    far_count, near_count = lax.axis_size("far"), lax.axis_size("near")
    x_count, core_count = lax.axis_size("x"), lax.axis_size("core")
    role_count = lax.axis_size("role")
    rows, width = payload.shape
    groups = near_count * x_count
    high, half = rows // groups, width // core_count
    blocks = block_of.reshape(x_count, far_count, near_count, core_count)
    holds = [jnp.any(blocks == panel, axis=(0, 2, 3)) for panel in range(2)]
    apart = jnp.logical_not(jnp.any(holds[0] & holds[1]))
    blocks = lax.dynamic_index_in_dim(blocks, lax.axis_index("far"), 1, keepdims=False)
    blocks = blocks.transpose(1, 0, 2).reshape(-1, 1, 1)
    pieces = payload.reshape(groups, high, core_count, half)
    pieces = pieces.transpose(0, 2, 1, 3).reshape(groups * core_count, high, half)
    seen = exchange(pieces, ("near", "x", "core"))
    own = jnp.concatenate(
        [jnp.sum(jnp.where(blocks == panel, seen, 0.0), axis=0) for panel in range(2)], axis=0
    )
    parts = [known] + [
        lax.ppermute(known, "role", [(i, (i + step) % role_count) for i in range(role_count)])
        for step in range(1, role_count)
    ]

    def gathered(strip):
        seen = copies_from(strip, ("far", "near"))
        return seen.reshape(far_count, near_count, *strip.shape)

    def whole_strips(own):
        return jnp.sum(gathered(own), axis=0)

    def half_strips(own):
        seen = gathered(own[:high] + own[high:])
        chosen = [
            jnp.sum(jnp.where(held.reshape(-1, 1, 1, 1), seen, 0.0), axis=0) for held in holds
        ]
        return jnp.concatenate(chosen, axis=1)

    strip = lax.cond(apart, half_strips, whole_strips, own)
    strip, *parts = lax.optimization_barrier((strip, *parts))
    mine = copies_from(strip, ("role", "x"))
    other = lax.ppermute(mine, "core", [(0, 1), (1, 0)])
    return mine, other, parts


def on_device(embeddings, earlier_factor, block_of):
    columns = embeddings.shape[0] // lax.axis_size("role")
    role = lax.axis_index("role")
    own_points = lax.dynamic_slice_in_dim(embeddings, role * columns, columns, 0)
    known = earlier_factor.T
    payload = jnp.concatenate([own_points, known], axis=1)
    mine, other, parts = broadcast_panels(payload, known, block_of)
    return finish(block_of, mine, other, embeddings, parts).transpose(2, 0, 1)


def solution(mesh):
    finer = Mesh(
        mesh.devices.reshape(mesh.shape["role"], 4, 4, 4, 2), ("role", *ROWS)
    )
    placed = (P(ROWS, None), P(ROWS, "role"), P())
    return jax.shard_map(
        on_device, mesh=finer, in_specs=placed, out_specs=P(ROWS, None, "role"), check_vma=False
    )
```
